128 devices in a mesh: blk: 8 (over x, core), mem: 16 (over z, y).
Axes of the slice: x: 4, y: 4, z: 4, core: 2. Of those that a mesh axis runs over, the one named last changes fastest.
Arguments:
- queries: bfloat16 [16, 2048, 3072], P('mem', 'blk'), may hold values from -17 to 17
- segment_pairs: bfloat16 [16, 2048, 2, 3072], P('mem', 'blk'), may hold values from -11 to 11
- memory_pairs: bfloat16 [512, 128, 2, 3072], P('mem', None, None, 'blk'), may hold values from -11 to 11
- block_lists: int32 [16, 16, 3], P('mem'), may hold values from 0 to 511, as said below
- gate_bias: float32 [24], replicated, may hold values from -2.5 to 2.5
Outputs:
- attended: bfloat16 [16, 2048, 3072], P('mem', 'blk')
The draws below stay inside these ranges and needn't reach their ends.
Inputs may be any that keep to these rules, and one draw needn't show every extreme that they name: `block_lists`: owner o holds ids o * 32 to (o + 1) * 32 - 1. Of the 48 ids listed by one segment, counted with repetition, at most 5 fall to one owner; segment s lists exactly 5 ids of owner (s + shift) mod 16, with one shift for all segments. An id may repeat within a list.
All inputs are finite; a program needn't handle non-finite values.
Results may differ from the reference program's by a relative error of at most 0.0048.
Values may be sent and summed in bfloat16 or wider, within the bound.
A program may use at most 192 MiB of HBM per device.

```python
import jax
import jax.numpy as jnp
from jax import lax

H = 24
HD = 128
BLK = 128
MEMK = 3
MEM_DEV = 32
SEGS = 16
SEGLEN = 2048
QB_SEG = 16
MEMBLOCKS = 512
CAP = 5


def draw_queries(key, part):
    shape = (SEGS, SEGLEN, H * HD)
    base_key = jax.random.fold_in(key, 11)
    result = jnp.clip(jax.random.normal(base_key, shape, jnp.float32), -5.0, 5.0)
    return result.astype(jnp.bfloat16)


def draw_pairs(key, salt, leading, length):
    shape = (leading, length, 2, H * HD)
    base_key = jax.random.fold_in(key, salt)
    normal = jnp.clip(jax.random.normal(base_key, shape, jnp.float32), -3.0, 3.0)
    scales = jnp.array([3.0, 1.0], jnp.float32).reshape(1, 1, 2, 1)
    result = normal * scales
    return result.astype(jnp.bfloat16)


def draw_segment_pairs(key, part):
    return draw_pairs(key, 23, SEGS, SEGLEN)


def draw_memory_pairs(key, part):
    return draw_pairs(key, 29, MEMBLOCKS, BLK)


def one_segment(segment_key, hot_owner):
    request_count = QB_SEG * MEMK
    slot_owner = jnp.arange(SEGS * CAP, dtype=jnp.int32) // CAP
    order_key, mix_key, local_key = jax.random.split(segment_key, 3)
    slot_order = jax.random.permutation(order_key, SEGS * CAP).astype(jnp.int32)
    slot_score = jnp.where(slot_owner == hot_owner, 0, SEGS * CAP) + slot_order
    picked = jnp.argsort(slot_score)[:request_count]
    owners = slot_owner[picked]
    local_ids = jax.random.randint(local_key, (request_count,), 0, MEM_DEV, dtype=jnp.int32)
    local_ids = local_ids.at[0].set(0).at[1].set(MEM_DEV - 1)
    block_ids = owners * MEM_DEV + local_ids
    return jax.random.permutation(mix_key, block_ids).reshape(QB_SEG, MEMK)


def draw_block_lists(key, part):
    shift_key, segment_key = jax.random.split(jax.random.fold_in(key, 31))
    hot_shift = jax.random.randint(shift_key, (), 0, SEGS, dtype=jnp.int32)
    hot_owners = (jnp.arange(SEGS, dtype=jnp.int32) + hot_shift) % SEGS
    segment_keys = jax.random.split(segment_key, SEGS)
    return jax.vmap(one_segment)(segment_keys, hot_owners).astype(jnp.int32)


def setup_inputs(seed: int = 0) -> dict:
    key_list = jax.random.split(jax.random.key(seed), 6)
    return {
        "queries": draw_queries(jax.random.fold_in(key_list[5], 71), 0),
        "segment_pairs": draw_segment_pairs(jax.random.fold_in(key_list[5], 71), 0),
        "memory_pairs": draw_memory_pairs(jax.random.fold_in(key_list[5], 71), 0),
        "block_lists": draw_block_lists(jax.random.fold_in(key_list[5], 71), 0),
        "gate_bias": jnp.clip(jax.random.uniform(key_list[4], (H,), jnp.float32, -2.5, 2.5), -2.5, 2.5),
    }


masked_score = -1.0e30


def softmax_mix(scores, value_rows):
    highest = jnp.max(scores, axis=2, keepdims=True)
    weights = jnp.exp(scores - highest)
    totals = jnp.sum(weights, axis=2)
    rounded = lax.optimization_barrier(weights.astype(jnp.bfloat16)).astype(jnp.float32)
    numerator = jnp.einsum("thj,jhd->thd", rounded, value_rows.astype(jnp.float32))
    return numerator / totals[:, :, None]


def local_segment(segment_queries, segment_pairs):
    length = segment_queries.shape[0]
    head_count = segment_queries.shape[1] // HD
    query_rows = segment_queries.reshape(length, head_count, HD).astype(jnp.float32)
    key_rows = segment_pairs[:, 0, :].reshape(length, head_count, HD).astype(jnp.float32)
    value_rows = segment_pairs[:, 1, :].reshape(length, head_count, HD)
    row_count = min(512, length)
    score_scale = HD ** -0.5

    def one_block(row_start):
        query_part = lax.dynamic_slice_in_dim(query_rows, row_start, row_count, 0)
        scores = jnp.einsum("thd,jhd->thj", query_part, key_rows) * score_scale
        positions = row_start + jnp.arange(row_count, dtype=jnp.int32)
        allowed = jnp.arange(length, dtype=jnp.int32)[None, :] <= positions[:, None]
        scores = jnp.where(allowed[:, None, :], scores, masked_score)
        return softmax_mix(scores, value_rows)

    starts = jnp.arange(length // row_count, dtype=jnp.int32) * row_count
    mixed = lax.map(one_block, starts)
    return mixed.reshape(length, head_count * HD)


def memory_segment(segment_queries, segment_lists, memory_pairs):
    head_count = segment_queries.shape[1] // HD
    score_scale = HD ** -0.5
    query_blocks = segment_queries.reshape(QB_SEG, BLK, head_count, HD)

    def one_block(operands):
        block_queries, block_ids = operands
        chosen = jnp.take(memory_pairs, block_ids.astype(jnp.int32), axis=0)
        key_rows = chosen[:, :, 0, :].reshape(MEMK * BLK, head_count, HD).astype(jnp.float32)
        value_rows = chosen[:, :, 1, :].reshape(MEMK * BLK, head_count, HD)
        scores = jnp.einsum("thd,jhd->thj", block_queries.astype(jnp.float32), key_rows) * score_scale
        return softmax_mix(scores, value_rows).astype(jnp.bfloat16)

    mixed = lax.map(one_block, (query_blocks, segment_lists))
    return mixed.reshape(QB_SEG * BLK, head_count * HD)


def reference(queries, segment_pairs, memory_pairs, block_lists, gate_bias):
    def local_one(operands):
        return local_segment(operands[0], operands[1])

    def memory_one(operands):
        return memory_segment(operands[0], operands[1], memory_pairs)

    local_out = lax.map(local_one, (queries, segment_pairs))
    memory_out = lax.map(memory_one, (queries, block_lists))
    memory_out = lax.optimization_barrier(memory_out).astype(jnp.float32)
    gate_cols = jnp.repeat(jax.nn.sigmoid(gate_bias.astype(jnp.float32)), HD)
    attended = gate_cols * memory_out + (1.0 - gate_cols) * local_out
    return attended.astype(jnp.bfloat16)
```

```python
import math

import jax
import jax.numpy as jnp
from jax import lax
from jax.experimental import pallas as pl
from jax.experimental.pallas import tpu as pltpu
from jax.sharding import PartitionSpec as P

HD = 128
BLK = 128
MEMK = 3
CAP = 5
SIDE = 4
NBLK = 8
MESH = pl.DeviceIdType.MESH
EXPONENT = HD ** (-0.5) * math.log2(math.e)
MASKED = -1e30
NT = (((1,), (1,)), ((), ()))


def request_slots(block_lists, per_owner, owner_count):
    flat_ids = block_lists.reshape(-1)
    count = flat_ids.shape[0]
    owners = flat_ids // per_owner
    local_ids = flat_ids - owners * per_owner
    order = jnp.arange(count, dtype=jnp.int32)
    earlier = (owners[:, None] == owners[None, :]) & (order[None, :] < order[:, None])
    ranks = jnp.sum(earlier.astype(jnp.int32), axis=1)
    slot_ids = owners * CAP + ranks
    matches = slot_ids[:, None] == jnp.arange(owner_count * CAP, dtype=jnp.int32)[None, :]
    table = jnp.sum(jnp.where(matches, local_ids[:, None], 0), axis=0)
    return table.reshape(owner_count, CAP), owners, ranks


def kernel(heads, tokens, per_owner, table, listed, bias, q_in, seg, mem, out, relay_k, relay_v, *scratch):
    (wide, keys, vals, ak, av, kst, vst, qr, kr, vr, lo, ob) = scratch[:12]
    rk = scratch[12 : 12 + heads]
    rv = scratch[12 + heads : 12 + 2 * heads]
    (x_send, x_recv, m_send, m_recv, o_send, o_recv, here) = scratch[12 + 2 * heads :]
    width = heads * HD
    b = lax.axis_index("blk")
    m = lax.axis_index("mem")
    x, core = b // 2, lax.rem(b, 2)
    z, y = m // SIDE, lax.rem(m, SIDE)

    def z_peer(d):
        return {"blk": b, "mem": lax.rem(z + d, SIDE) * SIDE + y}

    def y_peer(d):
        return {"blk": b, "mem": z * SIDE + lax.rem(y + d, SIDE)}

    def x_index(rel):
        return lax.rem(x + rel // 2, SIDE) * 2 + lax.rem(core + rel, 2)

    def x_peer(rel):
        return {"blk": x_index(rel), "mem": m}

    barrier = pltpu.get_barrier_semaphore()
    for d in range(1, SIDE):
        pl.semaphore_signal(barrier, inc=1, device_id=z_peer(d), device_id_type=MESH)
        pl.semaphore_signal(barrier, inc=1, device_id=y_peer(d), device_id_type=MESH)
    for rel in range(1, NBLK):
        pl.semaphore_signal(barrier, inc=1, device_id=x_peer(rel), device_id_type=MESH)

    def split_pair(rows, slot):
        count = rows.shape[0]
        view = wide.at[slot]
        view[pl.ds(0, 2 * count), :] = rows.reshape(2 * count, HD).astype(jnp.float32)
        first = view[pl.ds(0, count, stride=2), :].astype(jnp.bfloat16)
        second = view[pl.ds(1, count, stride=2), :].astype(jnp.bfloat16)
        return first, second

    def pack(h):
        @pl.loop(0, per_owner // 4)
        def _(i):
            for u in range(4):
                e = i * 4 + u
                first, second = split_pair(mem[e, :, :, h * HD : (h + 1) * HD], u)
                keys[e] = first
                vals[e] = second

        @pl.loop(0, SIDE * SIDE)
        def _(t):
            dz, dy = t // SIDE, lax.rem(t, SIDE)
            seg_id = lax.rem(z + dz, SIDE) * SIDE + lax.rem(y + dy, SIDE)
            for r in range(CAP):
                e = table[seg_id * CAP + r]
                ak[h, dz, dy, r] = keys[e]
                av[h, dy, dz, r] = vals[e]

        for r in range(CAP):
            e = table[m * CAP + r]
            rk[h][0, 0, r] = keys[e]
            rv[h][0, 0, r] = vals[e]

    def remote(src, dst, send, recv, peer):
        return pltpu.make_async_remote_copy(
            src_ref=src, dst_ref=dst, send_sem=send, recv_sem=recv, device_id=peer, device_id_type=MESH
        )

    paths = ((ak, relay_k, rk, z_peer, y_peer), (av, relay_v, rv, y_peer, z_peer))

    def memory_copy(p, h, kind, d):
        src, relay, land, first, second = paths[p]
        sems = (m_send.at[p, h, kind, d], m_recv.at[p, h, kind, d])
        if kind == 0:
            return remote(src.at[h, d, pl.ds(1, 3)], relay.at[h, d, pl.ds(1, 3)], *sems, first(d))
        if kind == 1:
            return remote(src.at[h, d, 0], land[h].at[0, d], *sems, first(d))
        if kind == 2:
            return remote(src.at[h, 0, d], land[h].at[d, 0], *sems, second(d))
        return remote(relay.at[h, pl.ds(1, 3), d], land[h].at[d, pl.ds(1, 3)], *sems, second(d))

    def start_first(h):
        for kind in (0, 1, 2):
            for d in (2, 1, 3):
                for p in range(2):
                    memory_copy(p, h, kind, d).start()

    def relay_on(h):
        for p in range(2):
            for d in range(1, SIDE):
                memory_copy(p, h, 0, d).wait_recv()
        for d in (2, 1, 3):
            for p in range(2):
                memory_copy(p, h, 3, d).start()

    def wait_memory(h):
        for kind in (1, 2, 3):
            for d in range(1, SIDE):
                for p in range(2):
                    memory_copy(p, h, kind, d).wait_recv()

    def query_copy(rel):
        cols = pl.ds(pl.multiple_of(x_index(rel) * width, HD), width)
        return remote(q_in.at[0, :, cols], qr.at[b], x_send.at[0, rel], x_recv.at[0, rel], x_peer(rel))

    def key_copy(rel):
        return remote(kst.at[x_index(rel)], kr.at[b], x_send.at[1, rel], x_recv.at[1, rel], x_peer(rel))

    def value_copy(rel):
        return remote(vst.at[x_index(rel)], vr.at[b], x_send.at[2, rel], x_recv.at[2, rel], x_peer(rel))

    def own_copies():
        cols = pl.ds(pl.multiple_of(b * width, HD), width)
        return (
            pltpu.make_async_copy(q_in.at[0, :, cols], qr.at[b], here.at[0]),
            pltpu.make_async_copy(kst.at[b], kr.at[b], here.at[1]),
            pltpu.make_async_copy(vst.at[b], vr.at[b], here.at[2]),
        )

    pack(0)
    pl.semaphore_wait(barrier, 2 * (SIDE - 1) + NBLK - 1)
    start_first(0)
    for rel in range(1, NBLK):
        query_copy(rel).start()

    @pl.loop(0, NBLK)
    def _(j):
        for h in range(heads):
            cols = pl.ds(pl.multiple_of(j * width + h * HD, HD), HD)
            first, second = split_pair(seg[0, :, :, cols], h)
            kst[j, h] = first
            vst[j, h] = second

    for rel in range(1, NBLK):
        key_copy(rel).start()
        value_copy(rel).start()
    own = own_copies()
    for copy in own:
        copy.start()
    for h in range(1, heads):
        pack(h)
        start_first(h)
    relay_on(0)
    for copy in own:
        copy.wait()
    for rel in range(1, NBLK):
        query_copy(rel).wait()
        key_copy(rel).wait()
        value_copy(rel).wait()

    def local_rows(i):
        queries = [qr[i, :, h * HD : (h + 1) * HD] for h in range(heads)]
        below = lax.broadcasted_iota(jnp.int32, (tokens, tokens), 1) <= lax.broadcasted_iota(
            jnp.int32, (tokens, tokens), 0
        )

        def absorb(j, state, diagonal):
            following = []
            for h in range(heads):
                top, total, acc = state[h]
                scores = lax.dot_general(queries[h], kr[j, h], NT, preferred_element_type=jnp.float32)
                if diagonal:
                    scores = jnp.where(below, scores, MASKED)
                raised = jnp.maximum(top, jnp.max(scores, axis=1, keepdims=True))
                factor = jnp.exp2((top - raised) * EXPONENT)
                weights = jnp.exp2((scores - raised) * EXPONENT)
                total = total * factor + jnp.sum(weights, axis=1, keepdims=True)
                acc = acc * factor + jnp.dot(
                    weights.astype(jnp.bfloat16), vr[j, h], preferred_element_type=jnp.float32
                )
                following.append((raised, total, acc))
            return tuple(following)

        state = tuple(
            (
                jnp.full((tokens, 1), MASKED, jnp.float32),
                jnp.zeros((tokens, 1), jnp.float32),
                jnp.zeros((tokens, HD), jnp.float32),
            )
            for _ in range(heads)
        )
        state = absorb(i, state, True)
        state = lax.fori_loop(0, i, lambda j, s: absorb(j, s, False), state)
        for h in range(heads):
            lo[h, i] = state[h][2] / state[h][1]

    def output_copy(h, rel):
        cols = pl.ds(pl.multiple_of(b * width + h * HD, HD), HD)
        return remote(
            ob.at[h, x_index(rel)], out.at[0, :, cols], o_send.at[h, rel], o_recv.at[h, rel], x_peer(rel)
        )

    def own_output(h):
        cols = pl.ds(pl.multiple_of(b * width + h * HD, HD), HD)
        return pltpu.make_async_copy(ob.at[h, b], out.at[0, :, cols], here.at[3 + h])

    def mixed_rows(h, i, gate):
        for half in range(tokens // BLK):
            rows = pl.ds(half * BLK, BLK)
            first = (i * (tokens // BLK) + half) * MEMK
            ids = [[listed[c * listed_count + first + k] for c in range(3)] for k in range(MEMK)]
            queries = qr[i, rows, h * HD : (h + 1) * HD]
            scores = [
                lax.dot_general(
                    queries, rk[h][dy, dz, r], NT, preferred_element_type=jnp.float32
                )
                for dz, dy, r in ids
            ]
            top = jnp.max(scores[0], axis=1, keepdims=True)
            for s in scores[1:]:
                top = jnp.maximum(top, jnp.max(s, axis=1, keepdims=True))
            weights = [jnp.exp2((s - top) * EXPONENT) for s in scores]
            total = sum(jnp.sum(w, axis=1, keepdims=True) for w in weights)
            acc = sum(
                jnp.dot(w.astype(jnp.bfloat16), rv[h][dz, dy, r], preferred_element_type=jnp.float32)
                for w, (dz, dy, r) in zip(weights, ids)
            )
            recalled = (acc / total).astype(jnp.bfloat16).astype(jnp.float32)
            ob[h, i, rows] = (gate * recalled + (1.0 - gate) * lo[h, i, rows]).astype(jnp.bfloat16)

    listed_count = listed.shape[0] // 3

    for h in range(1, heads - 1):
        relay_on(h)
    pl.loop(0, NBLK - 2)(local_rows)
    relay_on(heads - 1)
    pl.loop(NBLK - 2, NBLK)(local_rows)

    for h in range(heads):
        wait_memory(h)
        gate = 1.0 / (1.0 + jnp.exp(-jnp.full((1, HD), bias[b * heads + h], jnp.float32)))

        @pl.loop(1, NBLK)
        def _(rel):
            mixed_rows(h, x_index(rel), gate)
            output_copy(h, rel).start()

        mixed_rows(h, b, gate)
        own_output(h).start()

    for h in range(heads):
        for p in range(2):
            for kind in range(4):
                for d in range(1, SIDE):
                    memory_copy(p, h, kind, d).wait_send()
        own_output(h).wait()
        for rel in range(1, NBLK):
            output_copy(h, rel).wait()


def on_device(queries, segment_pairs, memory_pairs, block_lists, gate_bias):
    tokens, full_width = queries.shape[1:]
    blk_count = lax.axis_size("blk")
    owner_count = lax.axis_size("mem")
    heads = full_width // blk_count // HD
    per_owner = memory_pairs.shape[0]
    own_table, owners, ranks = request_slots(block_lists[0], per_owner, owner_count)
    incoming = lax.all_to_all(own_table, "mem", split_axis=0, concat_axis=0, tiled=True)
    here = lax.axis_index("mem")
    dz = (here // SIDE - owners // SIDE) % SIDE
    dy = (here % SIDE - owners % SIDE) % SIDE
    listed = jnp.concatenate([dz, dy, ranks])
    bf16, f32 = jnp.bfloat16, jnp.float32
    slots = (SIDE, SIDE, CAP, BLK, HD)
    vmem, smem, anywhere = pltpu.VMEM, pltpu.SMEM, pl.ANY
    dma = pltpu.SemaphoreType.DMA
    body = lambda *refs: kernel(heads, tokens, per_owner, *refs)
    result = pl.pallas_call(
        body,
        out_shape=[
            jax.ShapeDtypeStruct(queries.shape, bf16),
            jax.ShapeDtypeStruct((heads,) + slots, bf16),
            jax.ShapeDtypeStruct((heads,) + slots, bf16),
        ],
        in_specs=[pl.BlockSpec(memory_space=smem)] * 3
        + [pl.BlockSpec(memory_space=anywhere)]
        + [pl.BlockSpec(memory_space=vmem)] * 2,
        out_specs=[pl.BlockSpec(memory_space=anywhere)] * 3,
        scratch_shapes=[
            vmem((4, 2 * tokens, HD), f32),
            vmem((per_owner, BLK, HD), bf16),
            vmem((per_owner, BLK, HD), bf16),
            vmem((heads,) + slots, bf16),
            vmem((heads,) + slots, bf16),
            vmem((blk_count, heads, tokens, HD), bf16),
            vmem((blk_count, heads, tokens, HD), bf16),
            vmem((blk_count, tokens, heads * HD), bf16),
            vmem((blk_count, heads, tokens, HD), bf16),
            vmem((blk_count, heads, tokens, HD), bf16),
            vmem((heads, blk_count, tokens, HD), f32),
            vmem((heads, blk_count, tokens, HD), bf16),
        ]
        + [vmem(slots, bf16)] * (2 * heads)
        + [
            dma((3, blk_count)),
            dma((3, blk_count)),
            dma((2, heads, 4, SIDE)),
            dma((2, heads, 4, SIDE)),
            dma((heads, blk_count)),
            dma((heads, blk_count)),
            dma((3 + heads,)),
        ],
        compiler_params=pltpu.CompilerParams(
            collective_id=0, has_side_effects=True, vmem_limit_bytes=67043328
        ),
        name="attend",
    )(incoming.reshape(-1), listed, gate_bias, queries, segment_pairs, memory_pairs)
    return result[0]


def solution(mesh):
    in_specs = (
        P("mem", "blk", None),
        P("mem", "blk", None, None),
        P("mem", None, None, "blk"),
        P("mem", None, None),
        P(),
    )
    out_specs = P("mem", "blk", None)
    return jax.shard_map(
        on_device, mesh=mesh, in_specs=in_specs, out_specs=out_specs, check_vma=False
    )
```

```python
import math

import jax
import jax.numpy as jnp
from jax import lax
from jax.experimental import pallas as pl
from jax.experimental.pallas import tpu as pltpu
from jax.sharding import PartitionSpec as P

HD = 128
BLK = 128
MEMK = 3
CAP = 5
SIDE = 4
NBLK = 8
PARTS = 4
MESH = pl.DeviceIdType.MESH
EXPONENT = HD ** (-0.5) * math.log2(math.e)
MASKED = -1e30
NT = (((1,), (1,)), ((), ()))


def request_slots(block_lists, per_owner, owner_count):
    flat_ids = block_lists.reshape(-1)
    count = flat_ids.shape[0]
    owners = flat_ids // per_owner
    local_ids = flat_ids - owners * per_owner
    order = jnp.arange(count, dtype=jnp.int32)
    earlier = (owners[:, None] == owners[None, :]) & (order[None, :] < order[:, None])
    ranks = jnp.sum(earlier.astype(jnp.int32), axis=1)
    owner_rows = owners[:, None, None] == jnp.arange(owner_count, dtype=jnp.int32)[None, :, None]
    rank_lanes = ranks[:, None, None] == jnp.arange(HD, dtype=jnp.int32)[None, None, :]
    table = jnp.sum(jnp.where(owner_rows & rank_lanes, local_ids[:, None, None], 0), axis=0)
    here = lax.axis_index("mem")
    dz = (here // SIDE - owners // SIDE) % SIDE
    dy = (here % SIDE - owners % SIDE) % SIDE
    return table.reshape(owner_count, 1, HD), (dz * SIDE + dy) * 8 + ranks


def kernel(
    heads, tokens, per_owner, own_table, listed, bias, q_in, seg_in, mem_in, out, relay_k, relay_v, *scratch
):
    (wide, keys, vals, ak, av, kst, vst, qr, kr, vr, lo, ob, seg, mem, tables) = scratch[:15]
    rk = scratch[15 : 15 + heads]
    rv = scratch[15 + heads : 15 + 2 * heads]
    (table, x_send, x_recv, m_send, m_recv, o_send, o_recv, t_send, t_recv, here, loads) = scratch[
        15 + 2 * heads :
    ]
    width = heads * HD
    b = lax.axis_index("blk")
    m = lax.axis_index("mem")
    x, core = b // 2, lax.rem(b, 2)
    z, y = m // SIDE, lax.rem(m, SIDE)

    def z_peer(d):
        return {"blk": b, "mem": lax.rem(z + d, SIDE) * SIDE + y}

    def y_peer(d):
        return {"blk": b, "mem": z * SIDE + lax.rem(y + d, SIDE)}

    def x_index(rel):
        return lax.rem(x + rel // 2, SIDE) * 2 + lax.rem(core + rel, 2)

    def x_peer(rel):
        return {"blk": x_index(rel), "mem": m}

    def m_index(t):
        return lax.rem(z + t // SIDE, SIDE) * SIDE + lax.rem(y + lax.rem(t, SIDE), SIDE)

    def m_peer(t):
        return {"blk": b, "mem": m_index(t)}

    part = per_owner // PARTS
    mem_loads = [
        pltpu.make_async_copy(
            mem_in.at[pl.ds(c * part, part)], mem.at[pl.ds(c * part, part)], loads.at[c]
        )
        for c in range(PARTS)
    ]
    seg_load = pltpu.make_async_copy(seg_in.at[0], seg, loads.at[PARTS])
    for copy in mem_loads:
        copy.start()
    seg_load.start()

    barrier = pltpu.get_barrier_semaphore()
    for t in range(1, SIDE * SIDE):
        pl.semaphore_signal(barrier, inc=1, device_id=m_peer(t), device_id_type=MESH)
    for rel in range(1, NBLK):
        pl.semaphore_signal(barrier, inc=1, device_id=x_peer(rel), device_id_type=MESH)

    def split_pair(rows, slot):
        count = rows.shape[0]
        view = wide.at[slot]
        view[pl.ds(0, 2 * count), :] = rows.reshape(2 * count, HD).astype(jnp.float32)
        first = view[pl.ds(0, count, stride=2), :].astype(jnp.bfloat16)
        second = view[pl.ds(1, count, stride=2), :].astype(jnp.bfloat16)
        return first, second

    def split_blocks(h, start, count):
        @pl.loop(0, count // 4)
        def _(i):
            for u in range(4):
                e = start + i * 4 + u
                first, second = split_pair(mem[e, :, :, h * HD : (h + 1) * HD], u)
                keys[e] = first
                vals[e] = second

    def pack(h):
        @pl.loop(0, SIDE * SIDE)
        def _(t):
            dz, dy = t // SIDE, lax.rem(t, SIDE)
            seg_id = m_index(t)
            for r in range(CAP):
                e = table[seg_id, 0, r]
                ak[h, dz, dy, r] = keys[e]
                av[h, dy, dz, r] = vals[e]

        for r in range(CAP):
            e = table[m, 0, r]
            rk[h][0, 0, r] = keys[e]
            rv[h][0, 0, r] = vals[e]

    def remote(src, dst, send, recv, peer):
        return pltpu.make_async_remote_copy(
            src_ref=src, dst_ref=dst, send_sem=send, recv_sem=recv, device_id=peer, device_id_type=MESH
        )

    paths = ((ak, relay_k, rk, z_peer, y_peer), (av, relay_v, rv, y_peer, z_peer))

    def memory_copy(p, h, kind, d):
        src, relay, land, first, second = paths[p]
        sems = (m_send.at[p, h, kind, d], m_recv.at[p, h, kind, d])
        if kind == 0:
            return remote(src.at[h, d, pl.ds(1, 3)], relay.at[h, d, pl.ds(1, 3)], *sems, first(d))
        if kind == 1:
            return remote(src.at[h, d, 0], land[h].at[0, d], *sems, first(d))
        if kind == 2:
            return remote(src.at[h, 0, d], land[h].at[d, 0], *sems, second(d))
        return remote(relay.at[h, pl.ds(1, 3), d], land[h].at[d, pl.ds(1, 3)], *sems, second(d))

    def start_first(h):
        for kind in (0, 1, 2):
            for d in (2, 1, 3):
                for p in range(2):
                    memory_copy(p, h, kind, d).start()

    def relay_on(h):
        for p in range(2):
            for d in range(1, SIDE):
                memory_copy(p, h, 0, d).wait_recv()
        for d in (2, 1, 3):
            for p in range(2):
                memory_copy(p, h, 3, d).start()

    def wait_memory(h):
        for kind in (1, 2, 3):
            for d in range(1, SIDE):
                for p in range(2):
                    memory_copy(p, h, kind, d).wait_recv()

    def query_copy(rel):
        cols = pl.ds(pl.multiple_of(x_index(rel) * width, HD), width)
        return remote(q_in.at[0, :, cols], qr.at[b], x_send.at[0, rel], x_recv.at[0, rel], x_peer(rel))

    def key_copy(rel):
        return remote(kst.at[x_index(rel)], kr.at[b], x_send.at[1, rel], x_recv.at[1, rel], x_peer(rel))

    def value_copy(rel):
        return remote(vst.at[x_index(rel)], vr.at[b], x_send.at[2, rel], x_recv.at[2, rel], x_peer(rel))

    def own_copies():
        cols = pl.ds(pl.multiple_of(b * width, HD), width)
        return (
            pltpu.make_async_copy(q_in.at[0, :, cols], qr.at[b], here.at[0]),
            pltpu.make_async_copy(kst.at[b], kr.at[b], here.at[1]),
            pltpu.make_async_copy(vst.at[b], vr.at[b], here.at[2]),
        )

    def table_copy(t):
        return remote(own_table.at[m_index(t)], tables.at[m], t_send.at[t], t_recv.at[t], m_peer(t))

    own_row = pltpu.make_async_copy(own_table.at[m], tables.at[m], loads.at[PARTS + 1])
    to_scalars = pltpu.make_async_copy(tables, table, loads.at[PARTS + 2])
    own_row.start()
    pl.semaphore_wait(barrier, SIDE * SIDE - 1 + NBLK - 1)
    for t in range(SIDE * SIDE - 1, 0, -1):
        table_copy(t).start()
    for rel in range(1, NBLK):
        query_copy(rel).start()
    for c, copy in enumerate(mem_loads):
        copy.wait()
        split_blocks(0, c * part, part)
    own_row.wait()
    for t in range(1, SIDE * SIDE):
        table_copy(t).wait()
    to_scalars.start()
    to_scalars.wait()
    pack(0)
    start_first(0)
    seg_load.wait()

    @pl.loop(0, NBLK)
    def _(j):
        for h in range(heads):
            cols = pl.ds(pl.multiple_of(j * width + h * HD, HD), HD)
            first, second = split_pair(seg[:, :, cols], h)
            kst[j, h] = first
            vst[j, h] = second

    for rel in range(1, NBLK):
        key_copy(rel).start()
        value_copy(rel).start()
    own = own_copies()
    for copy in own:
        copy.start()
    for h in range(1, heads):
        split_blocks(h, 0, per_owner)
        pack(h)
        start_first(h)
    relay_on(0)
    for copy in own:
        copy.wait()
    for rel in range(1, NBLK):
        query_copy(rel).wait()
        key_copy(rel).wait()
        value_copy(rel).wait()

    def local_rows(i):
        queries = [qr[i, :, h * HD : (h + 1) * HD] for h in range(heads)]
        below = lax.broadcasted_iota(jnp.int32, (tokens, tokens), 1) <= lax.broadcasted_iota(
            jnp.int32, (tokens, tokens), 0
        )

        def absorb(j, state, diagonal):
            following = []
            for h in range(heads):
                top, total, acc = state[h]
                scores = lax.dot_general(queries[h], kr[j, h], NT, preferred_element_type=jnp.float32)
                if diagonal:
                    scores = jnp.where(below, scores, MASKED)
                raised = jnp.maximum(top, jnp.max(scores, axis=1, keepdims=True))
                factor = jnp.exp2((top - raised) * EXPONENT)
                weights = jnp.exp2((scores - raised) * EXPONENT)
                total = total * factor + jnp.sum(weights, axis=1, keepdims=True)
                acc = acc * factor + jnp.dot(
                    weights.astype(jnp.bfloat16), vr[j, h], preferred_element_type=jnp.float32
                )
                following.append((raised, total, acc))
            return tuple(following)

        state = tuple(
            (
                jnp.full((tokens, 1), MASKED, jnp.float32),
                jnp.zeros((tokens, 1), jnp.float32),
                jnp.zeros((tokens, HD), jnp.float32),
            )
            for _ in range(heads)
        )
        state = absorb(i, state, True)
        state = lax.fori_loop(0, i, lambda j, s: absorb(j, s, False), state)
        for h in range(heads):
            lo[h, i] = state[h][2] / state[h][1]

    def output_copy(h, rel):
        cols = pl.ds(pl.multiple_of(b * width + h * HD, HD), HD)
        return remote(
            ob.at[h, x_index(rel)], out.at[0, :, cols], o_send.at[h, rel], o_recv.at[h, rel], x_peer(rel)
        )

    def own_output(h):
        cols = pl.ds(pl.multiple_of(b * width + h * HD, HD), HD)
        return pltpu.make_async_copy(ob.at[h, b], out.at[0, :, cols], here.at[3 + h])

    def mixed_rows(h, i, gate):
        for half in range(tokens // BLK):
            rows = pl.ds(half * BLK, BLK)
            first = (i * (tokens // BLK) + half) * MEMK
            codes = [listed[first + k] for k in range(MEMK)]
            ids = [(c // (8 * SIDE), lax.rem(c // 8, SIDE), lax.rem(c, 8)) for c in codes]
            queries = qr[i, rows, h * HD : (h + 1) * HD]
            scores = [
                lax.dot_general(
                    queries, rk[h][dy, dz, r], NT, preferred_element_type=jnp.float32
                )
                for dz, dy, r in ids
            ]
            top = jnp.max(scores[0], axis=1, keepdims=True)
            for s in scores[1:]:
                top = jnp.maximum(top, jnp.max(s, axis=1, keepdims=True))
            weights = [jnp.exp2((s - top) * EXPONENT) for s in scores]
            total = sum(jnp.sum(w, axis=1, keepdims=True) for w in weights)
            acc = sum(
                jnp.dot(w.astype(jnp.bfloat16), rv[h][dz, dy, r], preferred_element_type=jnp.float32)
                for w, (dz, dy, r) in zip(weights, ids)
            )
            recalled = (acc / total).astype(jnp.bfloat16).astype(jnp.float32)
            ob[h, i, rows] = (gate * recalled + (1.0 - gate) * lo[h, i, rows]).astype(jnp.bfloat16)

    for h in range(1, heads - 1):
        relay_on(h)
    pl.loop(0, NBLK - 2)(local_rows)
    relay_on(heads - 1)
    pl.loop(NBLK - 2, NBLK)(local_rows)

    for h in range(heads):
        wait_memory(h)
        gate = 1.0 / (1.0 + jnp.exp(-jnp.full((1, HD), bias[b * heads + h], jnp.float32)))

        @pl.loop(1, NBLK)
        def _(rel):
            mixed_rows(h, x_index(rel), gate)
            output_copy(h, rel).start()

        mixed_rows(h, b, gate)
        own_output(h).start()

    for h in range(heads):
        for p in range(2):
            for kind in range(4):
                for d in range(1, SIDE):
                    memory_copy(p, h, kind, d).wait_send()
        own_output(h).wait()
        for rel in range(1, NBLK):
            output_copy(h, rel).wait()


def on_device(queries, segment_pairs, memory_pairs, block_lists, gate_bias):
    tokens, full_width = queries.shape[1:]
    blk_count = lax.axis_size("blk")
    owner_count = lax.axis_size("mem")
    heads = full_width // blk_count // HD
    per_owner = memory_pairs.shape[0]
    own_table, listed = request_slots(block_lists[0], per_owner, owner_count)
    bf16, f32 = jnp.bfloat16, jnp.float32
    slots = (SIDE, SIDE, CAP, BLK, HD)
    vmem, smem, anywhere = pltpu.VMEM, pltpu.SMEM, pl.ANY
    dma = pltpu.SemaphoreType.DMA
    body = lambda *refs: kernel(heads, tokens, per_owner, *refs)
    result = pl.pallas_call(
        body,
        out_shape=[
            jax.ShapeDtypeStruct(queries.shape, bf16),
            jax.ShapeDtypeStruct((heads,) + slots, bf16),
            jax.ShapeDtypeStruct((heads,) + slots, bf16),
        ],
        in_specs=[pl.BlockSpec(memory_space=vmem)]
        + [pl.BlockSpec(memory_space=smem)] * 2
        + [pl.BlockSpec(memory_space=anywhere)] * 3,
        out_specs=[pl.BlockSpec(memory_space=anywhere)] * 3,
        scratch_shapes=[
            vmem((4, 2 * tokens, HD), f32),
            vmem((per_owner, BLK, HD), bf16),
            vmem((per_owner, BLK, HD), bf16),
            vmem((heads,) + slots, bf16),
            vmem((heads,) + slots, bf16),
            vmem((blk_count, heads, tokens, HD), bf16),
            vmem((blk_count, heads, tokens, HD), bf16),
            vmem((blk_count, tokens, heads * HD), bf16),
            vmem((blk_count, heads, tokens, HD), bf16),
            vmem((blk_count, heads, tokens, HD), bf16),
            vmem((heads, blk_count, tokens, HD), f32),
            vmem((heads, blk_count, tokens, HD), bf16),
            vmem(segment_pairs.shape[1:], bf16),
            vmem(memory_pairs.shape, bf16),
            vmem((owner_count, 1, HD), jnp.int32),
        ]
        + [vmem(slots, bf16)] * (2 * heads)
        + [
            smem((owner_count, 1, HD), jnp.int32),
            dma((3, blk_count)),
            dma((3, blk_count)),
            dma((2, heads, 4, SIDE)),
            dma((2, heads, 4, SIDE)),
            dma((heads, blk_count)),
            dma((heads, blk_count)),
            dma((owner_count,)),
            dma((owner_count,)),
            dma((3 + heads,)),
            dma((PARTS + 3,)),
        ],
        compiler_params=pltpu.CompilerParams(
            collective_id=0, has_side_effects=True, vmem_limit_bytes=67043328
        ),
        name="attend",
    )(own_table, listed, gate_bias, queries, segment_pairs, memory_pairs)
    return result[0]


def solution(mesh):
    in_specs = (
        P("mem", "blk", None),
        P("mem", "blk", None, None),
        P("mem", None, None, "blk"),
        P("mem", None, None),
        P(),
    )
    out_specs = P("mem", "blk", None)
    return jax.shard_map(
        on_device, mesh=mesh, in_specs=in_specs, out_specs=out_specs, check_vma=False
    )
```

```python
import math

import jax
import jax.numpy as jnp
from jax import lax
from jax.experimental import pallas as pl
from jax.experimental.pallas import tpu as pltpu
from jax.sharding import PartitionSpec as P

HD = 128
BLK = 128
MEMK = 3
CAP = 5
SIDE = 4
NBLK = 8
PARTS = 4
NEAR_FIRST = (1, 3, 2)
MESH = pl.DeviceIdType.MESH
EXPONENT = HD ** (-0.5) * math.log2(math.e)
MASKED = -1e30
NT = (((1,), (1,)), ((), ()))


def request_slots(listed, per_owner, owner_count):
    owners = listed // per_owner
    local_ids = listed - owners * per_owner
    order = lax.broadcasted_iota(jnp.int32, listed.shape, 0) * listed.shape[1]
    order = order + lax.broadcasted_iota(jnp.int32, listed.shape, 1)
    earlier = (owners[:, :, None, None] == owners) & (order < order[:, :, None, None])
    ranks = jnp.sum(earlier.astype(jnp.int32), axis=(2, 3))
    cells = (owners * HD + ranks)[:, :, None, None]
    rows = lax.broadcasted_iota(jnp.int32, (owner_count, HD), 0) * HD
    rows = rows + lax.broadcasted_iota(jnp.int32, (owner_count, HD), 1)
    table = jnp.sum(jnp.where(cells == rows, local_ids[:, :, None, None], 0), axis=(0, 1))
    here = lax.axis_index("mem")
    dz = (here // SIDE - owners // SIDE) % SIDE
    dy = (here % SIDE - owners % SIDE) % SIDE
    return table.reshape(owner_count, 1, HD), (dz * SIDE + dy) * 8 + ranks


def kernel(
    heads, tokens, per_owner, own_table, listed, bias, q_in, seg_in, mem_in, out, relay_k, relay_v, *scratch
):
    (wide, keys, vals, ak, av, kst, vst, qr, kr, vr, lo, ob, seg, mem, tables) = scratch[:15]
    rk = scratch[15 : 15 + heads]
    rv = scratch[15 + heads : 15 + 2 * heads]
    (table, x_send, x_recv, m_send, m_recv, o_send, o_recv, t_send, t_recv, here, loads) = scratch[
        15 + 2 * heads :
    ]
    width = heads * HD
    b = lax.axis_index("blk")
    m = lax.axis_index("mem")
    x, core = b // 2, lax.rem(b, 2)
    z, y = m // SIDE, lax.rem(m, SIDE)

    def z_peer(d):
        return {"blk": b, "mem": lax.rem(z + d, SIDE) * SIDE + y}

    def y_peer(d):
        return {"blk": b, "mem": z * SIDE + lax.rem(y + d, SIDE)}

    def x_index(rel):
        return lax.rem(x + rel // 2, SIDE) * 2 + lax.rem(core + rel, 2)

    def x_peer(rel):
        return {"blk": x_index(rel), "mem": m}

    def m_index(t):
        return lax.rem(z + t // SIDE, SIDE) * SIDE + lax.rem(y + lax.rem(t, SIDE), SIDE)

    def m_peer(t):
        return {"blk": b, "mem": m_index(t)}

    part = per_owner // PARTS
    mem_loads = [
        pltpu.make_async_copy(
            mem_in.at[pl.ds(c * part, part)], mem.at[pl.ds(c * part, part)], loads.at[c]
        )
        for c in range(PARTS)
    ]
    seg_load = pltpu.make_async_copy(seg_in.at[0], seg, loads.at[PARTS])
    for copy in mem_loads:
        copy.start()
    seg_load.start()

    barrier = pltpu.get_barrier_semaphore()
    for t in range(1, SIDE * SIDE):
        pl.semaphore_signal(barrier, inc=1, device_id=m_peer(t), device_id_type=MESH)
    for rel in range(1, NBLK):
        pl.semaphore_signal(barrier, inc=1, device_id=x_peer(rel), device_id_type=MESH)

    def split_pair(rows, slot):
        count = rows.shape[0]
        view = wide.at[slot]
        view[pl.ds(0, 2 * count), :] = rows.reshape(2 * count, HD).astype(jnp.float32)
        first = view[pl.ds(0, count, stride=2), :].astype(jnp.bfloat16)
        second = view[pl.ds(1, count, stride=2), :].astype(jnp.bfloat16)
        return first, second

    def split_blocks(h, start, count):
        @pl.loop(0, count // 4)
        def _(i):
            for u in range(4):
                e = start + i * 4 + u
                first, second = split_pair(mem[e, :, :, h * HD : (h + 1) * HD], u)
                keys[e] = first
                vals[e] = second

    def pack(h):
        @pl.loop(0, SIDE * SIDE)
        def _(t):
            dz, dy = t // SIDE, lax.rem(t, SIDE)
            seg_id = m_index(t)
            for r in range(CAP):
                e = table[seg_id, 0, r]
                ak[h, dz, dy, r] = keys[e]
                av[h, dy, dz, r] = vals[e]

        for r in range(CAP):
            e = table[m, 0, r]
            rk[h][0, 0, r] = keys[e]
            rv[h][0, 0, r] = vals[e]

    def remote(src, dst, send, recv, peer):
        return pltpu.make_async_remote_copy(
            src_ref=src, dst_ref=dst, send_sem=send, recv_sem=recv, device_id=peer, device_id_type=MESH
        )

    paths = ((ak, relay_k, rk, z_peer, y_peer), (av, relay_v, rv, y_peer, z_peer))

    def memory_copy(p, h, kind, d):
        src, relay, land, first, second = paths[p]
        sems = (m_send.at[p, h, kind, d], m_recv.at[p, h, kind, d])
        if kind == 0:
            return remote(src.at[h, d, pl.ds(1, 3)], relay.at[h, d, pl.ds(1, 3)], *sems, first(d))
        if kind == 1:
            return remote(src.at[h, d, 0], land[h].at[0, d], *sems, first(d))
        if kind == 2:
            return remote(src.at[h, 0, d], land[h].at[d, 0], *sems, second(d))
        return remote(relay.at[h, pl.ds(1, 3), d], land[h].at[d, pl.ds(1, 3)], *sems, second(d))

    def start_first(h):
        for kind in (0, 1, 2):
            for d in NEAR_FIRST:
                for p in range(2):
                    memory_copy(p, h, kind, d).start()

    def relay_on(h):
        for p in range(2):
            for d in range(1, SIDE):
                memory_copy(p, h, 0, d).wait_recv()
        for d in NEAR_FIRST:
            for p in range(2):
                memory_copy(p, h, 3, d).start()

    def wait_memory(h):
        for kind in (1, 2, 3):
            for d in range(1, SIDE):
                for p in range(2):
                    memory_copy(p, h, kind, d).wait_recv()

    def query_copy(rel):
        cols = pl.ds(pl.multiple_of(x_index(rel) * width, HD), width)
        return remote(q_in.at[0, :, cols], qr.at[b], x_send.at[0, rel], x_recv.at[0, rel], x_peer(rel))

    def key_copy(rel):
        return remote(kst.at[x_index(rel)], kr.at[b], x_send.at[1, rel], x_recv.at[1, rel], x_peer(rel))

    def value_copy(rel):
        return remote(vst.at[x_index(rel)], vr.at[b], x_send.at[2, rel], x_recv.at[2, rel], x_peer(rel))

    def own_copies():
        cols = pl.ds(pl.multiple_of(b * width, HD), width)
        return (
            pltpu.make_async_copy(q_in.at[0, :, cols], qr.at[b], here.at[0]),
            pltpu.make_async_copy(kst.at[b], kr.at[b], here.at[1]),
            pltpu.make_async_copy(vst.at[b], vr.at[b], here.at[2]),
        )

    def table_copy(t):
        return remote(own_table.at[m_index(t)], tables.at[m], t_send.at[t], t_recv.at[t], m_peer(t))

    own_row = pltpu.make_async_copy(own_table.at[m], tables.at[m], loads.at[PARTS + 1])
    to_scalars = pltpu.make_async_copy(tables, table, loads.at[PARTS + 2])
    own_row.start()
    for c in range(PARTS // 2):
        mem_loads[c].wait()
        split_blocks(0, c * part, part)
    pl.semaphore_wait(barrier, SIDE * SIDE - 1 + NBLK - 1)
    for t in range(SIDE * SIDE - 1, 0, -1):
        table_copy(t).start()
    for rel in range(1, NBLK):
        query_copy(rel).start()
    for c in range(PARTS // 2, PARTS):
        mem_loads[c].wait()
        split_blocks(0, c * part, part)
    own_row.wait()
    for t in range(1, SIDE * SIDE):
        table_copy(t).wait()
    to_scalars.start()
    to_scalars.wait()
    pack(0)
    start_first(0)
    seg_load.wait()

    @pl.loop(0, NBLK)
    def _(j):
        for h in range(heads):
            cols = pl.ds(pl.multiple_of(j * width + h * HD, HD), HD)
            first, second = split_pair(seg[:, :, cols], h)
            kst[j, h] = first
            vst[j, h] = second

    for rel in range(1, NBLK):
        key_copy(rel).start()
        value_copy(rel).start()
    own = own_copies()
    for copy in own:
        copy.start()
    for h in range(1, heads):
        split_blocks(h, 0, per_owner)
        pack(h)
        start_first(h)
    relay_on(0)
    for copy in own:
        copy.wait()
    for rel in range(1, NBLK):
        query_copy(rel).wait()
        key_copy(rel).wait()
        value_copy(rel).wait()

    def local_rows(i):
        queries = [qr[i, :, h * HD : (h + 1) * HD] for h in range(heads)]
        below = lax.broadcasted_iota(jnp.int32, (tokens, tokens), 1) <= lax.broadcasted_iota(
            jnp.int32, (tokens, tokens), 0
        )

        def absorb(j, state, diagonal):
            following = []
            for h in range(heads):
                top, total, acc = state[h]
                scores = lax.dot_general(queries[h], kr[j, h], NT, preferred_element_type=jnp.float32)
                if diagonal:
                    scores = jnp.where(below, scores, MASKED)
                raised = jnp.maximum(top, jnp.max(scores, axis=1, keepdims=True))
                factor = jnp.exp2((top - raised) * EXPONENT)
                weights = jnp.exp2((scores - raised) * EXPONENT)
                total = total * factor + jnp.sum(weights, axis=1, keepdims=True)
                acc = acc * factor + jnp.dot(
                    weights.astype(jnp.bfloat16), vr[j, h], preferred_element_type=jnp.float32
                )
                following.append((raised, total, acc))
            return tuple(following)

        state = tuple(
            (
                jnp.full((tokens, 1), MASKED, jnp.float32),
                jnp.zeros((tokens, 1), jnp.float32),
                jnp.zeros((tokens, HD), jnp.float32),
            )
            for _ in range(heads)
        )
        state = absorb(i, state, True)
        state = lax.fori_loop(0, i, lambda j, s: absorb(j, s, False), state)
        for h in range(heads):
            lo[h, i] = state[h][2] / state[h][1]

    def output_copy(h, rel):
        cols = pl.ds(pl.multiple_of(b * width + h * HD, HD), HD)
        return remote(
            ob.at[h, x_index(rel)], out.at[0, :, cols], o_send.at[h, rel], o_recv.at[h, rel], x_peer(rel)
        )

    def own_output(h):
        cols = pl.ds(pl.multiple_of(b * width + h * HD, HD), HD)
        return pltpu.make_async_copy(ob.at[h, b], out.at[0, :, cols], here.at[3 + h])

    def mixed_rows(h, blocks, gate):
        halves = [(i, half) for i in blocks for half in range(tokens // BLK)]
        ids, scores = [], []
        for i, half in halves:
            block = i * (tokens // BLK) + half
            codes = [listed[k, block] for k in range(MEMK)]
            ids.append([(c // (8 * SIDE), lax.rem(c // 8, SIDE), lax.rem(c, 8)) for c in codes])
            queries = qr[i, pl.ds(half * BLK, BLK), h * HD : (h + 1) * HD]
            scores.append(
                [
                    lax.dot_general(queries, rk[h][dy, dz, r], NT, preferred_element_type=jnp.float32)
                    for dz, dy, r in ids[-1]
                ]
            )
        weights, totals = [], []
        for parts in scores:
            top = jnp.max(jnp.maximum(jnp.maximum(parts[0], parts[1]), parts[2]), axis=1, keepdims=True)
            weights.append([jnp.exp2((s - top) * EXPONENT) for s in parts])
            totals.append(jnp.sum(weights[-1][0] + weights[-1][1] + weights[-1][2], axis=1, keepdims=True))
        for (i, half), slots, parts, total in zip(halves, ids, weights, totals):
            acc = sum(
                jnp.dot(w.astype(jnp.bfloat16), rv[h][dz, dy, r], preferred_element_type=jnp.float32)
                for w, (dz, dy, r) in zip(parts, slots)
            )
            rows = pl.ds(half * BLK, BLK)
            recalled = (acc / total).astype(jnp.bfloat16).astype(jnp.float32)
            ob[h, i, rows] = (gate * recalled + (1.0 - gate) * lo[h, i, rows]).astype(jnp.bfloat16)

    for h in range(1, heads - 1):
        relay_on(h)
    pl.loop(0, NBLK - 2)(local_rows)
    relay_on(heads - 1)
    pl.loop(NBLK - 2, NBLK)(local_rows)

    for h in range(heads):
        wait_memory(h)
        gate = 1.0 / (1.0 + jnp.exp(-jnp.full((1, HD), bias[b * heads + h], jnp.float32)))

        @pl.loop(0, NBLK // 2 - 1)
        def _(pair):
            rels = (2 * pair + 2, 2 * pair + 3)
            mixed_rows(h, [x_index(rel) for rel in rels], gate)
            for rel in rels:
                output_copy(h, rel).start()

        mixed_rows(h, [x_index(1), b], gate)
        output_copy(h, 1).start()
        own_output(h).start()

    for h in range(heads):
        for p in range(2):
            for kind in range(4):
                for d in range(1, SIDE):
                    memory_copy(p, h, kind, d).wait_send()
        own_output(h).wait()
        for rel in range(1, NBLK):
            output_copy(h, rel).wait()


def settle_kernel(source, target, rows, sems):
    count = rows.shape[0]
    size = rows.shape[1]
    reads = [
        pltpu.make_async_copy(source.at[0, pl.ds(c * size, size)], rows.at[c], sems.at[0, c])
        for c in range(count)
    ]
    writes = [
        pltpu.make_async_copy(rows.at[c], target.at[0, pl.ds(c * size, size)], sems.at[1, c])
        for c in range(count)
    ]
    for copy in reads:
        copy.start()
    for read, write in zip(reads, writes):
        read.wait()
        write.start()
    for copy in writes:
        copy.wait()


def settle(x):
    count = 8
    return pl.pallas_call(
        settle_kernel,
        out_shape=jax.ShapeDtypeStruct(x.shape, x.dtype),
        in_specs=[pl.BlockSpec(memory_space=pl.ANY)],
        out_specs=pl.BlockSpec(memory_space=pl.ANY),
        scratch_shapes=[
            pltpu.VMEM((count, x.shape[1] // count, x.shape[2]), x.dtype),
            pltpu.SemaphoreType.DMA((2, count)),
        ],
        name="settle",
    )(x)


def on_device(queries, segment_pairs, memory_pairs, block_lists, gate_bias):
    tokens, full_width = queries.shape[1:]
    blk_count = lax.axis_size("blk")
    owner_count = lax.axis_size("mem")
    heads = full_width // blk_count // HD
    per_owner = memory_pairs.shape[0]
    own_table, listed = request_slots(block_lists[0].T, per_owner, owner_count)
    bf16, f32 = jnp.bfloat16, jnp.float32
    slots = (SIDE, SIDE, CAP, BLK, HD)
    vmem, smem, anywhere = pltpu.VMEM, pltpu.SMEM, pl.ANY
    dma = pltpu.SemaphoreType.DMA
    body = lambda *refs: kernel(heads, tokens, per_owner, *refs)
    result = pl.pallas_call(
        body,
        out_shape=[
            jax.ShapeDtypeStruct(queries.shape, bf16),
            jax.ShapeDtypeStruct((heads,) + slots, bf16),
            jax.ShapeDtypeStruct((heads,) + slots, bf16),
        ],
        in_specs=[pl.BlockSpec(memory_space=vmem)]
        + [pl.BlockSpec(memory_space=smem)] * 2
        + [pl.BlockSpec(memory_space=anywhere)] * 3,
        out_specs=[pl.BlockSpec(memory_space=anywhere)] * 3,
        scratch_shapes=[
            vmem((4, 2 * tokens, HD), f32),
            vmem((per_owner, BLK, HD), bf16),
            vmem((per_owner, BLK, HD), bf16),
            vmem((heads,) + slots, bf16),
            vmem((heads,) + slots, bf16),
            vmem((blk_count, heads, tokens, HD), bf16),
            vmem((blk_count, heads, tokens, HD), bf16),
            vmem((blk_count, tokens, heads * HD), bf16),
            vmem((blk_count, heads, tokens, HD), bf16),
            vmem((blk_count, heads, tokens, HD), bf16),
            vmem((heads, blk_count, tokens, HD), f32),
            vmem((heads, blk_count, tokens, HD), bf16),
            vmem(segment_pairs.shape[1:], bf16),
            vmem(memory_pairs.shape, bf16),
            vmem((owner_count, 1, HD), jnp.int32),
        ]
        + [vmem(slots, bf16)] * (2 * heads)
        + [
            smem((owner_count, 1, HD), jnp.int32),
            dma((3, blk_count)),
            dma((3, blk_count)),
            dma((2, heads, 4, SIDE)),
            dma((2, heads, 4, SIDE)),
            dma((heads, blk_count)),
            dma((heads, blk_count)),
            dma((owner_count,)),
            dma((owner_count,)),
            dma((3 + heads,)),
            dma((PARTS + 3,)),
        ],
        compiler_params=pltpu.CompilerParams(
            collective_id=0, has_side_effects=True, vmem_limit_bytes=67043328
        ),
        name="attend",
    )(own_table, listed, gate_bias, queries, segment_pairs, memory_pairs)
    return settle(result[0])


def solution(mesh):
    in_specs = (
        P("mem", "blk", None),
        P("mem", "blk", None, None),
        P("mem", None, None, "blk"),
        P("mem", None, None),
        P(),
    )
    out_specs = P("mem", "blk", None)
    return jax.shard_map(
        on_device, mesh=mesh, in_specs=in_specs, out_specs=out_specs, check_vma=False
    )
```

```python
import math

import jax
import jax.numpy as jnp
from jax import lax
from jax.experimental import pallas as pl
from jax.experimental.pallas import tpu as pltpu
from jax.sharding import PartitionSpec as P

HD = 128
BLK = 128
MEMK = 3
CAP = 5
SIDE = 4
NBLK = 8
PARTS = 4
NEAR_FIRST = (1, 3, 2)
MESH = pl.DeviceIdType.MESH
EXPONENT = HD ** (-0.5) * math.log2(math.e)
MASKED = -1e30
NT = (((1,), (1,)), ((), ()))


def request_slots(listed, per_owner, owner_count):
    owners = listed // per_owner
    local_ids = listed - owners * per_owner
    order = lax.broadcasted_iota(jnp.int32, listed.shape, 0) * listed.shape[1]
    order = order + lax.broadcasted_iota(jnp.int32, listed.shape, 1)
    earlier = (owners[:, :, None, None] == owners) & (order < order[:, :, None, None])
    ranks = jnp.sum(earlier.astype(jnp.int32), axis=(2, 3))
    cells = (owners * HD + ranks)[:, :, None, None]
    rows = lax.broadcasted_iota(jnp.int32, (owner_count, HD), 0) * HD
    rows = rows + lax.broadcasted_iota(jnp.int32, (owner_count, HD), 1)
    table = jnp.sum(jnp.where(cells == rows, local_ids[:, :, None, None], 0), axis=(0, 1))
    here = lax.axis_index("mem")
    dz = (here // SIDE - owners // SIDE) % SIDE
    dy = (here % SIDE - owners % SIDE) % SIDE
    return table.reshape(owner_count, 1, HD), (dz * SIDE + dy) * 8 + ranks


def kernel(
    heads, tokens, per_owner, own_table, listed, bias, q_in, seg_in, mem_in, out, relay_k, relay_v, *scratch
):
    (wide, keys, vals, ak, av, kst, vst, qr, kr, vr, lo, ob, seg, mem, tables) = scratch[:15]
    rk = scratch[15 : 15 + heads]
    rv = scratch[15 + heads : 15 + 2 * heads]
    (table, x_send, x_recv, m_send, m_recv, m_local, o_send, o_recv, t_send, t_recv, here, loads) = scratch[
        15 + 2 * heads :
    ]
    width = heads * HD
    b = lax.axis_index("blk")
    m = lax.axis_index("mem")
    x, core = b // 2, lax.rem(b, 2)
    z, y = m // SIDE, lax.rem(m, SIDE)

    def z_peer(d):
        return {"blk": b, "mem": lax.rem(z + d, SIDE) * SIDE + y}

    def y_peer(d):
        return {"blk": b, "mem": z * SIDE + lax.rem(y + d, SIDE)}

    def x_index(rel):
        return lax.rem(x + rel // 2, SIDE) * 2 + lax.rem(core + rel, 2)

    def x_peer(rel):
        return {"blk": x_index(rel), "mem": m}

    def m_index(t):
        return lax.rem(z + t // SIDE, SIDE) * SIDE + lax.rem(y + lax.rem(t, SIDE), SIDE)

    def m_peer(t):
        return {"blk": b, "mem": m_index(t)}

    part = per_owner // PARTS
    mem_loads = [
        pltpu.make_async_copy(
            mem_in.at[pl.ds(c * part, part)], mem.at[pl.ds(c * part, part)], loads.at[c]
        )
        for c in range(PARTS)
    ]
    seg_load = pltpu.make_async_copy(seg_in.at[0], seg, loads.at[PARTS])
    for copy in mem_loads:
        copy.start()
    seg_load.start()

    barrier = pltpu.get_barrier_semaphore()
    for t in range(1, SIDE * SIDE):
        pl.semaphore_signal(barrier, inc=1, device_id=m_peer(t), device_id_type=MESH)
    for rel in range(1, NBLK):
        pl.semaphore_signal(barrier, inc=1, device_id=x_peer(rel), device_id_type=MESH)

    def split_pair(rows, slot):
        count = rows.shape[0]
        view = wide.at[slot]
        view[pl.ds(0, 2 * count), :] = rows.reshape(2 * count, HD).astype(jnp.float32)
        first = view[pl.ds(0, count, stride=2), :].astype(jnp.bfloat16)
        second = view[pl.ds(1, count, stride=2), :].astype(jnp.bfloat16)
        return first, second

    def split_blocks(h, start, count):
        @pl.loop(0, count // 4)
        def _(i):
            for u in range(4):
                e = start + i * 4 + u
                first, second = split_pair(mem[e, :, :, h * HD : (h + 1) * HD], u)
                keys[e] = first
                vals[e] = second

    def pack(h):
        @pl.loop(0, SIDE * SIDE)
        def _(t):
            dz, dy = t // SIDE, lax.rem(t, SIDE)
            seg_id = m_index(t)
            for r in range(CAP):
                e = table[seg_id, 0, r]
                ak[h, dz, dy, r] = keys[e]
                av[h, dy, dz, r] = vals[e]

        for r in range(CAP):
            e = table[m, 0, r]
            rk[h][0, 0, r] = keys[e]
            rv[h][0, 0, r] = vals[e]

    def remote(src, dst, send, recv, peer):
        return pltpu.make_async_remote_copy(
            src_ref=src, dst_ref=dst, send_sem=send, recv_sem=recv, device_id=peer, device_id_type=MESH
        )

    paths = ((ak, relay_k, rk, z_peer, y_peer), (av, relay_v, rv, y_peer, z_peer))

    def memory_copy(p, h, kind, d):
        src, relay, land, first, second = paths[p]
        sems = (m_send.at[p, h, kind, d], m_recv.at[p, h, kind, d])
        if kind == 0:
            return remote(src.at[h, d], relay.at[h, d], *sems, first(d))
        return remote(relay.at[h, pl.ds(0, SIDE), d], land[h].at[d], *sems, second(d))

    def stage(p, h):
        src, relay = paths[p][:2]
        return pltpu.make_async_copy(src.at[h, 0], relay.at[h, 0], m_local.at[p, h, 0])

    def bring_home(p, h):
        relay, land = paths[p][1:3]
        source = relay.at[h, pl.ds(1, SIDE - 1), 0]
        return pltpu.make_async_copy(source, land[h].at[0, pl.ds(1, SIDE - 1)], m_local.at[p, h, 1])

    def start_first(h):
        for d in NEAR_FIRST:
            for p in range(2):
                memory_copy(p, h, 0, d).start()
        for p in range(2):
            stage(p, h).start()

    def relay_on(h):
        for p in range(2):
            stage(p, h).wait()
            for d in range(1, SIDE):
                memory_copy(p, h, 0, d).wait_recv()
        for d in NEAR_FIRST:
            for p in range(2):
                memory_copy(p, h, 1, d).start()
        for p in range(2):
            bring_home(p, h).start()

    def wait_memory(h):
        for p in range(2):
            bring_home(p, h).wait()
            for d in range(1, SIDE):
                memory_copy(p, h, 1, d).wait_recv()

    def query_copy(rel):
        cols = pl.ds(pl.multiple_of(x_index(rel) * width, HD), width)
        return remote(q_in.at[0, :, cols], qr.at[b], x_send.at[0, rel], x_recv.at[0, rel], x_peer(rel))

    def key_copy(rel):
        return remote(kst.at[x_index(rel)], kr.at[b], x_send.at[1, rel], x_recv.at[1, rel], x_peer(rel))

    def value_copy(rel):
        return remote(vst.at[x_index(rel)], vr.at[b], x_send.at[2, rel], x_recv.at[2, rel], x_peer(rel))

    def own_copies():
        cols = pl.ds(pl.multiple_of(b * width, HD), width)
        return (
            pltpu.make_async_copy(q_in.at[0, :, cols], qr.at[b], here.at[0]),
            pltpu.make_async_copy(kst.at[b], kr.at[b], here.at[1]),
            pltpu.make_async_copy(vst.at[b], vr.at[b], here.at[2]),
        )

    def table_copy(t):
        return remote(own_table.at[m_index(t)], tables.at[m], t_send.at[t], t_recv.at[t], m_peer(t))

    own_row = pltpu.make_async_copy(own_table.at[m], tables.at[m], loads.at[PARTS + 1])
    to_scalars = pltpu.make_async_copy(tables, table, loads.at[PARTS + 2])
    own_row.start()
    for c in range(PARTS // 2):
        mem_loads[c].wait()
        split_blocks(0, c * part, part)
    pl.semaphore_wait(barrier, SIDE * SIDE - 1 + NBLK - 1)
    for t in range(SIDE * SIDE - 1, 0, -1):
        table_copy(t).start()
    for rel in range(1, NBLK):
        query_copy(rel).start()
    for c in range(PARTS // 2, PARTS):
        mem_loads[c].wait()
        split_blocks(0, c * part, part)
    own_row.wait()
    for t in range(1, SIDE * SIDE):
        table_copy(t).wait()
    to_scalars.start()
    to_scalars.wait()
    pack(0)
    start_first(0)
    seg_load.wait()

    @pl.loop(0, NBLK)
    def _(j):
        for h in range(heads):
            cols = pl.ds(pl.multiple_of(j * width + h * HD, HD), HD)
            first, second = split_pair(seg[:, :, cols], h)
            kst[j, h] = first
            vst[j, h] = second

    for rel in range(1, NBLK):
        key_copy(rel).start()
        value_copy(rel).start()
    own = own_copies()
    for copy in own:
        copy.start()
    for h in range(1, heads):
        split_blocks(h, 0, per_owner)
        pack(h)
        start_first(h)
    relay_on(0)
    for copy in own:
        copy.wait()
    for rel in range(1, NBLK):
        query_copy(rel).wait()
        key_copy(rel).wait()
        value_copy(rel).wait()

    def local_rows(i):
        queries = [qr[i, :, h * HD : (h + 1) * HD] for h in range(heads)]
        below = lax.broadcasted_iota(jnp.int32, (tokens, tokens), 1) <= lax.broadcasted_iota(
            jnp.int32, (tokens, tokens), 0
        )

        def absorb(j, state, diagonal):
            following = []
            for h in range(heads):
                top, total, acc = state[h]
                scores = lax.dot_general(queries[h], kr[j, h], NT, preferred_element_type=jnp.float32)
                if diagonal:
                    scores = jnp.where(below, scores, MASKED)
                raised = jnp.maximum(top, jnp.max(scores, axis=1, keepdims=True))
                factor = jnp.exp2((top - raised) * EXPONENT)
                weights = jnp.exp2((scores - raised) * EXPONENT)
                total = total * factor + jnp.sum(weights, axis=1, keepdims=True)
                acc = acc * factor + jnp.dot(
                    weights.astype(jnp.bfloat16), vr[j, h], preferred_element_type=jnp.float32
                )
                following.append((raised, total, acc))
            return tuple(following)

        state = tuple(
            (
                jnp.full((tokens, 1), MASKED, jnp.float32),
                jnp.zeros((tokens, 1), jnp.float32),
                jnp.zeros((tokens, HD), jnp.float32),
            )
            for _ in range(heads)
        )
        state = absorb(i, state, True)
        state = lax.fori_loop(0, i, lambda j, s: absorb(j, s, False), state)
        for h in range(heads):
            lo[h, i] = state[h][2] / state[h][1]

    def output_copy(h, rel):
        cols = pl.ds(pl.multiple_of(b * width + h * HD, HD), HD)
        return remote(
            ob.at[h, x_index(rel)], out.at[0, :, cols], o_send.at[h, rel], o_recv.at[h, rel], x_peer(rel)
        )

    def own_output(h):
        cols = pl.ds(pl.multiple_of(b * width + h * HD, HD), HD)
        return pltpu.make_async_copy(ob.at[h, b], out.at[0, :, cols], here.at[3 + h])

    def mixed_rows(h, blocks, gate):
        halves = [(i, half) for i in blocks for half in range(tokens // BLK)]
        ids, scores = [], []
        for i, half in halves:
            block = i * (tokens // BLK) + half
            codes = [listed[k, block] for k in range(MEMK)]
            ids.append([(c // (8 * SIDE), lax.rem(c // 8, SIDE), lax.rem(c, 8)) for c in codes])
            queries = qr[i, pl.ds(half * BLK, BLK), h * HD : (h + 1) * HD]
            scores.append(
                [
                    lax.dot_general(queries, rk[h][dy, dz, r], NT, preferred_element_type=jnp.float32)
                    for dz, dy, r in ids[-1]
                ]
            )
        weights, totals = [], []
        for parts in scores:
            top = jnp.max(jnp.maximum(jnp.maximum(parts[0], parts[1]), parts[2]), axis=1, keepdims=True)
            weights.append([jnp.exp2((s - top) * EXPONENT) for s in parts])
            totals.append(jnp.sum(weights[-1][0] + weights[-1][1] + weights[-1][2], axis=1, keepdims=True))
        for (i, half), slots, parts, total in zip(halves, ids, weights, totals):
            acc = sum(
                jnp.dot(w.astype(jnp.bfloat16), rv[h][dz, dy, r], preferred_element_type=jnp.float32)
                for w, (dz, dy, r) in zip(parts, slots)
            )
            rows = pl.ds(half * BLK, BLK)
            recalled = (acc / total).astype(jnp.bfloat16).astype(jnp.float32)
            ob[h, i, rows] = (gate * recalled + (1.0 - gate) * lo[h, i, rows]).astype(jnp.bfloat16)

    for h in range(1, heads - 1):
        relay_on(h)
    pl.loop(0, NBLK - 2)(local_rows)
    relay_on(heads - 1)
    pl.loop(NBLK - 2, NBLK)(local_rows)

    for h in range(heads):
        wait_memory(h)
        gate = 1.0 / (1.0 + jnp.exp(-jnp.full((1, HD), bias[b * heads + h], jnp.float32)))

        @pl.loop(0, NBLK // 2 - 1)
        def _(pair):
            rels = (2 * pair + 2, 2 * pair + 3)
            mixed_rows(h, [x_index(rel) for rel in rels], gate)
            for rel in rels:
                output_copy(h, rel).start()

        mixed_rows(h, [x_index(1), b], gate)
        output_copy(h, 1).start()
        own_output(h).start()

    for h in range(heads):
        for p in range(2):
            for kind in range(2):
                for d in range(1, SIDE):
                    memory_copy(p, h, kind, d).wait_send()
        own_output(h).wait()
        for rel in range(1, NBLK):
            output_copy(h, rel).wait()


def settle_kernel(source, target, rows, sems):
    count = rows.shape[0]
    size = rows.shape[1]
    reads = [
        pltpu.make_async_copy(source.at[0, pl.ds(c * size, size)], rows.at[c], sems.at[0, c])
        for c in range(count)
    ]
    writes = [
        pltpu.make_async_copy(rows.at[c], target.at[0, pl.ds(c * size, size)], sems.at[1, c])
        for c in range(count)
    ]
    for copy in reads:
        copy.start()
    for read, write in zip(reads, writes):
        read.wait()
        write.start()
    for copy in writes:
        copy.wait()


def settle(x):
    count = 8
    return pl.pallas_call(
        settle_kernel,
        out_shape=jax.ShapeDtypeStruct(x.shape, x.dtype),
        in_specs=[pl.BlockSpec(memory_space=pl.ANY)],
        out_specs=pl.BlockSpec(memory_space=pl.ANY),
        scratch_shapes=[
            pltpu.VMEM((count, x.shape[1] // count, x.shape[2]), x.dtype),
            pltpu.SemaphoreType.DMA((2, count)),
        ],
        name="settle",
    )(x)


def on_device(queries, segment_pairs, memory_pairs, block_lists, gate_bias):
    tokens, full_width = queries.shape[1:]
    blk_count = lax.axis_size("blk")
    owner_count = lax.axis_size("mem")
    heads = full_width // blk_count // HD
    per_owner = memory_pairs.shape[0]
    own_table, listed = request_slots(block_lists[0].T, per_owner, owner_count)
    bf16, f32 = jnp.bfloat16, jnp.float32
    slots = (SIDE, SIDE, CAP, BLK, HD)
    vmem, smem, anywhere = pltpu.VMEM, pltpu.SMEM, pl.ANY
    dma = pltpu.SemaphoreType.DMA
    body = lambda *refs: kernel(heads, tokens, per_owner, *refs)
    result = pl.pallas_call(
        body,
        out_shape=[
            jax.ShapeDtypeStruct(queries.shape, bf16),
            jax.ShapeDtypeStruct((heads,) + slots, bf16),
            jax.ShapeDtypeStruct((heads,) + slots, bf16),
        ],
        in_specs=[pl.BlockSpec(memory_space=vmem)]
        + [pl.BlockSpec(memory_space=smem)] * 2
        + [pl.BlockSpec(memory_space=anywhere)] * 3,
        out_specs=[pl.BlockSpec(memory_space=anywhere)] * 3,
        scratch_shapes=[
            vmem((4, 2 * tokens, HD), f32),
            vmem((per_owner, BLK, HD), bf16),
            vmem((per_owner, BLK, HD), bf16),
            vmem((heads,) + slots, bf16),
            vmem((heads,) + slots, bf16),
            vmem((blk_count, heads, tokens, HD), bf16),
            vmem((blk_count, heads, tokens, HD), bf16),
            vmem((blk_count, tokens, heads * HD), bf16),
            vmem((blk_count, heads, tokens, HD), bf16),
            vmem((blk_count, heads, tokens, HD), bf16),
            vmem((heads, blk_count, tokens, HD), f32),
            vmem((heads, blk_count, tokens, HD), bf16),
            vmem(segment_pairs.shape[1:], bf16),
            vmem(memory_pairs.shape, bf16),
            vmem((owner_count, 1, HD), jnp.int32),
        ]
        + [vmem(slots, bf16)] * (2 * heads)
        + [
            smem((owner_count, 1, HD), jnp.int32),
            dma((3, blk_count)),
            dma((3, blk_count)),
            dma((2, heads, 2, SIDE)),
            dma((2, heads, 2, SIDE)),
            dma((2, heads, 2)),
            dma((heads, blk_count)),
            dma((heads, blk_count)),
            dma((owner_count,)),
            dma((owner_count,)),
            dma((3 + heads,)),
            dma((PARTS + 3,)),
        ],
        compiler_params=pltpu.CompilerParams(
            collective_id=0, has_side_effects=True, vmem_limit_bytes=67043328
        ),
        name="attend",
    )(own_table, listed, gate_bias, queries, segment_pairs, memory_pairs)
    return settle(result[0])


def solution(mesh):
    in_specs = (
        P("mem", "blk", None),
        P("mem", "blk", None, None),
        P("mem", None, None, "blk"),
        P("mem", None, None),
        P(),
    )
    out_specs = P("mem", "blk", None)
    return jax.shard_map(
        on_device, mesh=mesh, in_specs=in_specs, out_specs=out_specs, check_vma=False
    )
```

```python
import math

import jax
import jax.numpy as jnp
from jax import lax
from jax.experimental import pallas as pl
from jax.experimental.pallas import tpu as pltpu
from jax.sharding import PartitionSpec as P

HD = 128
BLK = 128
MEMK = 3
CAP = 5
SIDE = 4
NBLK = 8
PARTS = 4
NEAR_FIRST = (1, 3, 2)
MESH = pl.DeviceIdType.MESH
EXPONENT = HD ** (-0.5) * math.log2(math.e)
MASKED = -1e30
NT = (((1,), (1,)), ((), ()))


def request_slots(listed, per_owner, owner_count):
    owners = listed // per_owner
    local_ids = listed - owners * per_owner
    order = lax.broadcasted_iota(jnp.int32, listed.shape, 0) * listed.shape[1]
    order = order + lax.broadcasted_iota(jnp.int32, listed.shape, 1)
    earlier = (owners[:, :, None, None] == owners) & (order < order[:, :, None, None])
    ranks = jnp.sum(earlier.astype(jnp.int32), axis=(2, 3))
    cells = (owners * HD + ranks)[:, :, None, None]
    rows = lax.broadcasted_iota(jnp.int32, (owner_count, HD), 0) * HD
    rows = rows + lax.broadcasted_iota(jnp.int32, (owner_count, HD), 1)
    table = jnp.sum(jnp.where(cells == rows, local_ids[:, :, None, None], 0), axis=(0, 1))
    here = lax.axis_index("mem")
    dz = (here // SIDE - owners // SIDE) % SIDE
    dy = (here % SIDE - owners % SIDE) % SIDE
    return table.reshape(owner_count, 1, HD), (dz * SIDE + dy) * 8 + ranks


def kernel(
    heads, tokens, per_owner, own_table, listed, bias, q_in, seg_in, mem_in, out, relay_k, relay_v, *scratch
):
    (wide, keys, vals, ak, av, kst, vst, qr, kr, vr, lo, ob, seg, mem, tables) = scratch[:15]
    rk = scratch[15 : 15 + heads]
    rv = scratch[15 + heads : 15 + 2 * heads]
    (table, x_send, x_recv, m_send, m_recv, m_local, o_send, o_recv, t_send, t_recv, here, loads) = scratch[
        15 + 2 * heads :
    ]
    width = heads * HD
    b = lax.axis_index("blk")
    m = lax.axis_index("mem")
    x, core = b // 2, lax.rem(b, 2)
    z, y = m // SIDE, lax.rem(m, SIDE)

    def z_peer(d):
        return {"blk": b, "mem": lax.rem(z + d, SIDE) * SIDE + y}

    def y_peer(d):
        return {"blk": b, "mem": z * SIDE + lax.rem(y + d, SIDE)}

    def x_index(rel):
        return lax.rem(x + rel // 2, SIDE) * 2 + lax.rem(core + rel, 2)

    def x_peer(rel):
        return {"blk": x_index(rel), "mem": m}

    def m_index(t):
        return lax.rem(z + t // SIDE, SIDE) * SIDE + lax.rem(y + lax.rem(t, SIDE), SIDE)

    def m_peer(t):
        return {"blk": b, "mem": m_index(t)}

    part = per_owner // PARTS
    mem_loads = [
        pltpu.make_async_copy(
            mem_in.at[pl.ds(c * part, part)], mem.at[pl.ds(c * part, part)], loads.at[c]
        )
        for c in range(PARTS)
    ]
    seg_load = pltpu.make_async_copy(seg_in.at[0], seg, loads.at[PARTS])
    for copy in mem_loads:
        copy.start()
    seg_load.start()

    barrier = pltpu.get_barrier_semaphore()
    for t in range(1, SIDE * SIDE):
        pl.semaphore_signal(barrier, inc=1, device_id=m_peer(t), device_id_type=MESH)
    for rel in range(1, NBLK):
        pl.semaphore_signal(barrier, inc=1, device_id=x_peer(rel), device_id_type=MESH)

    def split_pair(rows, slot):
        count = rows.shape[0]
        view = wide.at[slot]
        view[pl.ds(0, 2 * count), :] = rows.reshape(2 * count, HD).astype(jnp.float32)
        first = view[pl.ds(0, count, stride=2), :].astype(jnp.bfloat16)
        second = view[pl.ds(1, count, stride=2), :].astype(jnp.bfloat16)
        return first, second

    def split_blocks(h, start, count):
        @pl.loop(0, count // 4)
        def _(i):
            for u in range(4):
                e = start + i * 4 + u
                first, second = split_pair(mem[e, :, :, h * HD : (h + 1) * HD], u)
                keys[e] = first
                vals[e] = second

    def pack_row(h, d):
        @pl.loop(0, SIDE)
        def _(other):
            over_z = m_index(d * SIDE + other)
            over_y = m_index(other * SIDE + d)
            for r in range(CAP):
                ak[h, d, other, r] = keys[table[over_z, 0, r]]
                av[h, d, other, r] = vals[table[over_y, 0, r]]

    def pack_own(h):
        for r in range(CAP):
            e = table[m, 0, r]
            rk[h][0, 0, r] = keys[e]
            rv[h][0, 0, r] = vals[e]

    def remote(src, dst, send, recv, peer):
        return pltpu.make_async_remote_copy(
            src_ref=src, dst_ref=dst, send_sem=send, recv_sem=recv, device_id=peer, device_id_type=MESH
        )

    paths = ((ak, relay_k, rk, z_peer, y_peer), (av, relay_v, rv, y_peer, z_peer))

    def memory_copy(p, h, kind, d):
        src, relay, land, first, second = paths[p]
        sems = (m_send.at[p, h, kind, d], m_recv.at[p, h, kind, d])
        if kind == 0:
            return remote(src.at[h, d], relay.at[h, d], *sems, first(d))
        return remote(relay.at[h, pl.ds(0, SIDE), d], land[h].at[d], *sems, second(d))

    def stage(p, h):
        src, relay = paths[p][:2]
        return pltpu.make_async_copy(src.at[h, 0], relay.at[h, 0], m_local.at[p, h, 0])

    def bring_home(p, h):
        relay, land = paths[p][1:3]
        source = relay.at[h, pl.ds(1, SIDE - 1), 0]
        return pltpu.make_async_copy(source, land[h].at[0, pl.ds(1, SIDE - 1)], m_local.at[p, h, 1])

    def start_first(h):
        for d in NEAR_FIRST:
            pack_row(h, d)
            for p in range(2):
                memory_copy(p, h, 0, d).start()
        pack_row(h, 0)
        for p in range(2):
            stage(p, h).start()
        pack_own(h)

    def relay_on(h):
        for p in range(2):
            stage(p, h).wait()
            for d in range(1, SIDE):
                memory_copy(p, h, 0, d).wait_recv()
        for d in NEAR_FIRST:
            for p in range(2):
                memory_copy(p, h, 1, d).start()
        for p in range(2):
            bring_home(p, h).start()

    def wait_memory(h):
        for p in range(2):
            bring_home(p, h).wait()
            for d in range(1, SIDE):
                memory_copy(p, h, 1, d).wait_recv()

    def query_copy(rel):
        cols = pl.ds(pl.multiple_of(x_index(rel) * width, HD), width)
        return remote(q_in.at[0, :, cols], qr.at[b], x_send.at[0, rel], x_recv.at[0, rel], x_peer(rel))

    def key_copy(rel):
        return remote(kst.at[x_index(rel)], kr.at[b], x_send.at[1, rel], x_recv.at[1, rel], x_peer(rel))

    def value_copy(rel):
        return remote(vst.at[x_index(rel)], vr.at[b], x_send.at[2, rel], x_recv.at[2, rel], x_peer(rel))

    def own_copies():
        cols = pl.ds(pl.multiple_of(b * width, HD), width)
        return (
            pltpu.make_async_copy(q_in.at[0, :, cols], qr.at[b], here.at[0]),
            pltpu.make_async_copy(kst.at[b], kr.at[b], here.at[1]),
            pltpu.make_async_copy(vst.at[b], vr.at[b], here.at[2]),
        )

    def table_copy(t):
        return remote(own_table.at[m_index(t)], tables.at[m], t_send.at[t], t_recv.at[t], m_peer(t))

    own_row = pltpu.make_async_copy(own_table.at[m], tables.at[m], loads.at[PARTS + 1])
    to_scalars = pltpu.make_async_copy(tables, table, loads.at[PARTS + 2])
    own_row.start()
    for c in range(PARTS // 2):
        mem_loads[c].wait()
        split_blocks(0, c * part, part)
    pl.semaphore_wait(barrier, SIDE * SIDE - 1 + NBLK - 1)
    for t in range(SIDE * SIDE - 1, 0, -1):
        table_copy(t).start()
    for rel in range(1, NBLK):
        query_copy(rel).start()
    for c in range(PARTS // 2, PARTS):
        mem_loads[c].wait()
        split_blocks(0, c * part, part)
    own_row.wait()
    for t in range(1, SIDE * SIDE):
        table_copy(t).wait()
    to_scalars.start()
    to_scalars.wait()
    start_first(0)
    seg_load.wait()

    @pl.loop(0, NBLK)
    def _(j):
        for h in range(heads):
            cols = pl.ds(pl.multiple_of(j * width + h * HD, HD), HD)
            first, second = split_pair(seg[:, :, cols], h)
            kst[j, h] = first
            vst[j, h] = second

    for rel in range(1, NBLK):
        key_copy(rel).start()
        value_copy(rel).start()
    own = own_copies()
    for copy in own:
        copy.start()
    for h in range(1, heads):
        split_blocks(h, 0, per_owner)
        start_first(h)
    relay_on(0)
    for copy in own:
        copy.wait()
    for rel in range(1, NBLK):
        query_copy(rel).wait()
        key_copy(rel).wait()
        value_copy(rel).wait()

    def local_rows(i):
        queries = [qr[i, :, h * HD : (h + 1) * HD] for h in range(heads)]
        below = lax.broadcasted_iota(jnp.int32, (tokens, tokens), 1) <= lax.broadcasted_iota(
            jnp.int32, (tokens, tokens), 0
        )

        def absorb(j, state, diagonal):
            following = []
            for h in range(heads):
                top, total, acc = state[h]
                scores = lax.dot_general(queries[h], kr[j, h], NT, preferred_element_type=jnp.float32)
                if diagonal:
                    scores = jnp.where(below, scores, MASKED)
                raised = jnp.maximum(top, jnp.max(scores, axis=1, keepdims=True))
                factor = jnp.exp2((top - raised) * EXPONENT)
                weights = jnp.exp2((scores - raised) * EXPONENT)
                total = total * factor + jnp.sum(weights, axis=1, keepdims=True)
                acc = acc * factor + jnp.dot(
                    weights.astype(jnp.bfloat16), vr[j, h], preferred_element_type=jnp.float32
                )
                following.append((raised, total, acc))
            return tuple(following)

        state = tuple(
            (
                jnp.full((tokens, 1), MASKED, jnp.float32),
                jnp.zeros((tokens, 1), jnp.float32),
                jnp.zeros((tokens, HD), jnp.float32),
            )
            for _ in range(heads)
        )
        state = absorb(i, state, True)
        state = lax.fori_loop(0, i, lambda j, s: absorb(j, s, False), state)
        for h in range(heads):
            lo[h, i] = state[h][2] / state[h][1]

    def output_copy(h, rel):
        cols = pl.ds(pl.multiple_of(b * width + h * HD, HD), HD)
        return remote(
            ob.at[h, x_index(rel)], out.at[0, :, cols], o_send.at[h, rel], o_recv.at[h, rel], x_peer(rel)
        )

    def own_output(h):
        cols = pl.ds(pl.multiple_of(b * width + h * HD, HD), HD)
        return pltpu.make_async_copy(ob.at[h, b], out.at[0, :, cols], here.at[3 + h])

    def mixed_rows(h, blocks, gate):
        halves = [(i, half) for i in blocks for half in range(tokens // BLK)]
        ids, scores = [], []
        for i, half in halves:
            block = i * (tokens // BLK) + half
            codes = [listed[k, block] for k in range(MEMK)]
            ids.append([(c // (8 * SIDE), lax.rem(c // 8, SIDE), lax.rem(c, 8)) for c in codes])
            queries = qr[i, pl.ds(half * BLK, BLK), h * HD : (h + 1) * HD]
            scores.append(
                [
                    lax.dot_general(queries, rk[h][dy, dz, r], NT, preferred_element_type=jnp.float32)
                    for dz, dy, r in ids[-1]
                ]
            )
        weights, totals = [], []
        for parts in scores:
            top = jnp.max(jnp.maximum(jnp.maximum(parts[0], parts[1]), parts[2]), axis=1, keepdims=True)
            weights.append([jnp.exp2((s - top) * EXPONENT) for s in parts])
            totals.append(jnp.sum(weights[-1][0] + weights[-1][1] + weights[-1][2], axis=1, keepdims=True))
        for (i, half), slots, parts, total in zip(halves, ids, weights, totals):
            acc = sum(
                jnp.dot(w.astype(jnp.bfloat16), rv[h][dz, dy, r], preferred_element_type=jnp.float32)
                for w, (dz, dy, r) in zip(parts, slots)
            )
            rows = pl.ds(half * BLK, BLK)
            recalled = (acc / total).astype(jnp.bfloat16).astype(jnp.float32)
            ob[h, i, rows] = (gate * recalled + (1.0 - gate) * lo[h, i, rows]).astype(jnp.bfloat16)

    for h in range(1, heads - 1):
        relay_on(h)
    pl.loop(0, NBLK - 2)(local_rows)
    relay_on(heads - 1)
    pl.loop(NBLK - 2, NBLK)(local_rows)

    for h in range(heads):
        wait_memory(h)
        gate = 1.0 / (1.0 + jnp.exp(-jnp.full((1, HD), bias[b * heads + h], jnp.float32)))

        @pl.loop(0, NBLK // 2 - 1)
        def _(pair):
            near = lax.rem(2 * pair + 2, NBLK - 2) + 2
            rels = (near, near + 1)
            mixed_rows(h, [x_index(rel) for rel in rels], gate)
            for rel in rels:
                output_copy(h, rel).start()

        mixed_rows(h, [x_index(1), b], gate)
        output_copy(h, 1).start()
        own_output(h).start()

    for h in range(heads):
        for p in range(2):
            for kind in range(2):
                for d in range(1, SIDE):
                    memory_copy(p, h, kind, d).wait_send()
        own_output(h).wait()
        for rel in range(1, NBLK):
            output_copy(h, rel).wait()


def settle_kernel(source, target, rows, sems):
    count = rows.shape[0]
    size = rows.shape[1]
    reads = [
        pltpu.make_async_copy(source.at[0, pl.ds(c * size, size)], rows.at[c], sems.at[0, c])
        for c in range(count)
    ]
    writes = [
        pltpu.make_async_copy(rows.at[c], target.at[0, pl.ds(c * size, size)], sems.at[1, c])
        for c in range(count)
    ]
    for copy in reads:
        copy.start()
    for read, write in zip(reads, writes):
        read.wait()
        write.start()
    for copy in writes:
        copy.wait()


def settle(x):
    count = 8
    return pl.pallas_call(
        settle_kernel,
        out_shape=jax.ShapeDtypeStruct(x.shape, x.dtype),
        in_specs=[pl.BlockSpec(memory_space=pl.ANY)],
        out_specs=pl.BlockSpec(memory_space=pl.ANY),
        scratch_shapes=[
            pltpu.VMEM((count, x.shape[1] // count, x.shape[2]), x.dtype),
            pltpu.SemaphoreType.DMA((2, count)),
        ],
        name="settle",
    )(x)


def on_device(queries, segment_pairs, memory_pairs, block_lists, gate_bias):
    tokens, full_width = queries.shape[1:]
    blk_count = lax.axis_size("blk")
    owner_count = lax.axis_size("mem")
    heads = full_width // blk_count // HD
    per_owner = memory_pairs.shape[0]
    own_table, listed = request_slots(block_lists[0].T, per_owner, owner_count)
    bf16, f32 = jnp.bfloat16, jnp.float32
    slots = (SIDE, SIDE, CAP, BLK, HD)
    vmem, smem, anywhere = pltpu.VMEM, pltpu.SMEM, pl.ANY
    dma = pltpu.SemaphoreType.DMA
    body = lambda *refs: kernel(heads, tokens, per_owner, *refs)
    result = pl.pallas_call(
        body,
        out_shape=[
            jax.ShapeDtypeStruct(queries.shape, bf16),
            jax.ShapeDtypeStruct((heads,) + slots, bf16),
            jax.ShapeDtypeStruct((heads,) + slots, bf16),
        ],
        in_specs=[pl.BlockSpec(memory_space=vmem)]
        + [pl.BlockSpec(memory_space=smem)] * 2
        + [pl.BlockSpec(memory_space=anywhere)] * 3,
        out_specs=[pl.BlockSpec(memory_space=anywhere)] * 3,
        scratch_shapes=[
            vmem((4, 2 * tokens, HD), f32),
            vmem((per_owner, BLK, HD), bf16),
            vmem((per_owner, BLK, HD), bf16),
            vmem((heads,) + slots, bf16),
            vmem((heads,) + slots, bf16),
            vmem((blk_count, heads, tokens, HD), bf16),
            vmem((blk_count, heads, tokens, HD), bf16),
            vmem((blk_count, tokens, heads * HD), bf16),
            vmem((blk_count, heads, tokens, HD), bf16),
            vmem((blk_count, heads, tokens, HD), bf16),
            vmem((heads, blk_count, tokens, HD), f32),
            vmem((heads, blk_count, tokens, HD), bf16),
            vmem(segment_pairs.shape[1:], bf16),
            vmem(memory_pairs.shape, bf16),
            vmem((owner_count, 1, HD), jnp.int32),
        ]
        + [vmem(slots, bf16)] * (2 * heads)
        + [
            smem((owner_count, 1, HD), jnp.int32),
            dma((3, blk_count)),
            dma((3, blk_count)),
            dma((2, heads, 2, SIDE)),
            dma((2, heads, 2, SIDE)),
            dma((2, heads, 2)),
            dma((heads, blk_count)),
            dma((heads, blk_count)),
            dma((owner_count,)),
            dma((owner_count,)),
            dma((3 + heads,)),
            dma((PARTS + 3,)),
        ],
        compiler_params=pltpu.CompilerParams(
            collective_id=0, has_side_effects=True, vmem_limit_bytes=67043328
        ),
        name="attend",
    )(own_table, listed, gate_bias, queries, segment_pairs, memory_pairs)
    return settle(result[0])


def solution(mesh):
    in_specs = (
        P("mem", "blk", None),
        P("mem", "blk", None, None),
        P("mem", None, None, "blk"),
        P("mem", None, None),
        P(),
    )
    out_specs = P("mem", "blk", None)
    return jax.shard_map(
        on_device, mesh=mesh, in_specs=in_specs, out_specs=out_specs, check_vma=False
    )
```
